512 devices in a mesh: seq: 64 (over z, x, core), head: 8 (over y).
Axes of the slice: x: 4, y: 8, z: 8, core: 2. Of those that a mesh axis runs over, the one named last changes fastest.
Arguments:
- queries: bfloat16 [64, 16384, 128], P('head', 'seq'), may hold values from -1.25 to 1.25
- key_rows: bfloat16 [64, 16384, 128], P('head', 'seq'), may hold values from -1.25 to 1.25
- value_rows: bfloat16 [64, 16384, 128], P('head', 'seq'), may hold values from -1.25 to 1.25
- grad_out: bfloat16 [64, 16384, 128], P('head', 'seq'), may hold values from -1.25 to 1.25
Outputs:
- grad_query: bfloat16 [64, 16384, 128], P('head', 'seq')
- grad_key: bfloat16 [64, 16384, 128], P('head', 'seq')
- grad_value: bfloat16 [64, 16384, 128], P('head', 'seq')
The draws below stay inside these ranges and needn't reach their ends.
All inputs are finite; a program needn't handle non-finite values.
Results may differ from the reference program's by a relative error of at most 0.0049.
Values sent between devices are 32-bit elements; how exact they have to be, the bound alone decides.
A program may use at most 192 MiB of HBM per device.

```python
import jax
import jax.numpy as jnp
from jax import lax

HD = 128
TILE = 256
HEADS = 64
TOKENS = 16384


def block_scale(own_key, dims, cuts, low, top_value):
    def one(axis_at, parts):
        draws = jax.random.uniform(jax.random.fold_in(jax.random.fold_in(own_key, 6), axis_at), (parts,), jnp.float32, low / len(cuts), top_value / len(cuts))
        return jnp.repeat(jnp.exp(draws), dims[axis_at] // parts).reshape((-1,) + (1,) * (len(dims) - axis_at - 1))

    loudness = one(*cuts[0])
    for cut in cuts[1:]:
        loudness = loudness * one(*cut)
    return loudness


def scatter_about(stream_key, extent, scale, reach, split=(), dtype=jnp.bfloat16):
    factor_of = block_scale(stream_key, extent, split, -0.22, 0.18) if split else 1.0
    entries = jax.random.normal(stream_key, extent, jnp.float32) * scale * factor_of
    return jnp.minimum(jnp.maximum(entries, -reach), reach).astype(dtype)


def setup_inputs(seed: int = 0) -> dict:
    splits = jax.random.split(jax.random.key(seed), 5)
    queries = scatter_about(splits[0], (HEADS, TOKENS, HD), ((HD * TOKENS) ** -0.16666667), 1.25, ((0, 8), (1, 64)))
    key_rows = scatter_about(splits[1], (HEADS, TOKENS, HD), ((HD * TOKENS) ** -0.16666667), 1.25, ((0, 8), (1, 64)))
    value_rows = scatter_about(splits[2], (HEADS, TOKENS, HD), ((HD * TOKENS) ** -0.16666667), 1.25, ((0, 8), (1, 64)))
    grad_out = scatter_about(splits[3], (HEADS, TOKENS, HD), ((HD * TOKENS) ** -0.16666667), 1.25, ((0, 8), (1, 64)))
    return {"queries": queries, "key_rows": key_rows, "value_rows": value_rows, "grad_out": grad_out}


def rounded(array):
    return lax.optimization_barrier(array.astype(jnp.bfloat16)).astype(jnp.float32)


def tile_grads(pieces):
    query_tile, key_tile, value_tile, grad_tile, earlier_states, later_states = pieces
    causal = jnp.arange(TILE)[:, None] >= jnp.arange(TILE)[None, :]
    out_scores = jnp.einsum("hta,hsa->hts", grad_tile, value_tile)
    out_scores = rounded(jnp.where(causal[None], out_scores, 0.0))
    attn_scores = jnp.einsum("hta,hsa->hts", query_tile, key_tile)
    attn_scores = rounded(jnp.where(causal[None], attn_scores, 0.0))
    grad_query = jnp.einsum("hts,hsa->hta", out_scores, key_tile) + jnp.einsum("htb,hab->hta", grad_tile, earlier_states)
    grad_key = jnp.einsum("hts,hta->hsa", out_scores, query_tile) + jnp.einsum("hsb,hab->hsa", value_tile, later_states)
    grad_value = jnp.einsum("hts,htb->hsb", attn_scores, grad_tile) + jnp.einsum("hsa,hab->hsb", key_tile, later_states)
    return (grad_query.astype(jnp.bfloat16), grad_key.astype(jnp.bfloat16), grad_value.astype(jnp.bfloat16))


def tiles_of(array):
    tile_count = TOKENS // TILE
    return array.astype(jnp.float32).reshape(HEADS, tile_count, TILE, HD).transpose(1, 0, 2, 3)


def reference(queries, key_rows, value_rows, grad_out):
    query_tiles = tiles_of(queries)
    key_tiles = tiles_of(key_rows)
    value_tiles = tiles_of(value_rows)
    grad_tiles = tiles_of(grad_out)
    key_state = jnp.einsum("jhsa,jhsb->jhab", key_tiles, value_tiles)
    query_state = jnp.einsum("jhta,jhtb->jhab", query_tiles, grad_tiles)
    zero_state = jnp.zeros((1, HEADS, HD, HD), jnp.float32)
    earlier_states = jnp.concatenate([zero_state, jnp.cumsum(key_state, 0)[:-1]], 0)
    later_states = jnp.concatenate([jnp.cumsum(query_state[::-1], 0)[::-1][1:], zero_state], 0)
    results = lax.map(tile_grads, (query_tiles, key_tiles, value_tiles, grad_tiles, rounded(earlier_states), rounded(later_states)))
    return tuple(result.transpose(1, 0, 2, 3).reshape(HEADS, TOKENS, HD) for result in results)
```

```python
import jax
import jax.numpy as jnp
from jax import lax
from jax.experimental import pallas as pl
from jax.experimental.pallas import tpu as pltpu
from jax.sharding import PartitionSpec as P

ROWS, COLS = 8, 4
CHUNKS = 4
F32, BF16 = jnp.float32, jnp.bfloat16
NN = (((1,), (0,)), ((), ()))
NT = (((1,), (1,)), ((), ()))
TN = (((0,), (0,)), ((), ()))


def dot(a, b, dims):
    return lax.dot_general(a, b, dims, preferred_element_type=F32)


def kernel(
    q_hbm, k_hbm, v_hbm, g_hbm,
    gq_hbm, gk_hbm, gv_hbm,
    inb, part, outb, state, core_in, chip, side_in, far_src, far_in, total, z_src, z_in,
    far_out_src, far_out, side_out_src, side_out, core_out_src, core_out,
    in_sem, out_sem,
    ci_s, ci_r, si_s, si_r, fi_s, fi_r, z_s, z_r, fo_s, fo_r, so_s, so_r, co_s, co_r,
):
    tile = inb.shape[3]
    width = inb.shape[4]
    rows = width // CHUNKS
    place = lax.axis_index("seq")
    c = lax.rem(place, 2)
    x = lax.rem(lax.div(place, 2), COLS)
    z = lax.div(place, 2 * COLS)
    o = 1 - c
    odd = lax.rem(x, 2)
    right = lax.div(x, 2)
    xa = x + 1 - 2 * odd
    xb = COLS - 1 - x

    def device(zz, xx, cc):
        return {"seq": (zz * COLS + xx) * 2 + cc}

    core, side, far = device(z, x, o), device(z, xa, c), device(z, xb, c)
    up, down = lax.rem(z + 1, ROWS), lax.rem(z + ROWS - 1, ROWS)

    loads = []
    for slot, parity in ((0, o), (1, c)):
        for i, source in ((1, k_hbm), (2, v_hbm), (0, q_hbm), (3, g_hbm)):
            copy = pltpu.make_async_copy(source.at[:, parity], inb.at[i, slot], in_sem.at[i, slot])
            copy.start()
            loads.append(copy)

    barrier = pltpu.get_barrier_semaphore()
    for peer in (core, side, far, device(up, x, c), device(down, x, c)):
        pl.semaphore_signal(barrier, inc=1, device_id=peer, device_id_type=pl.DeviceIdType.MESH)

    order = (COLS - 1 - xa, xa, COLS - 1 - x, x)

    def remote(src, dst, send, recv, peer):
        return pltpu.make_async_remote_copy(
            src_ref=src, dst_ref=dst, send_sem=send, recv_sem=recv, device_id=peer,
            device_id_type=pl.DeviceIdType.MESH,
        )

    sends = []

    def core_copy(w, j):
        return remote(state.at[w, 0, j], core_in.at[w, j], ci_s.at[w, j], ci_r.at[w, j], core)

    def side_copy(w, n, j):
        return remote(chip.at[w, j], side_in.at[w, n], si_s.at[w, n], si_r.at[w, n], side)

    def far_copy(w):
        return remote(far_src.at[w], far_in.at[w], fi_s.at[w], fi_r.at[w], far)

    def part_of(k):
        return pl.ds(k * rows, rows)

    def z_copy(w, k):
        peer = device(lax.rem(z + 1 - 2 * w + ROWS, ROWS), x, c)
        return remote(z_src.at[w, part_of(k)], z_in.at[w, part_of(k)], z_s.at[w, k], z_r.at[w, k], peer)

    def far_back(w, k):
        return remote(far_out_src.at[w, part_of(k)], far_out.at[w, part_of(k)], fo_s.at[w, k], fo_r.at[w, k], far)

    def side_back(w, n):
        return remote(side_out_src.at[w, n], side_out.at[w, n], so_s.at[w, n], so_r.at[w, n], side)

    def core_back(w, j):
        return remote(core_out_src.at[w, j], core_out.at[w, j], co_s.at[w, j], co_r.at[w, j], core)

    def start(copy):
        copy.start()
        sends.append(copy)

    def make_state(w, slot, j):
        a, b = ((1, 2), (0, 3))[w]
        state[w, slot, j] = dot(inb[a, slot, j], inb[b, slot, j], TN)

    for copy in loads[:4]:
        copy.wait()
    for n, j in enumerate(order):
        for w in (0, 1):
            make_state(w, 0, j)
        if n == 0:
            pl.semaphore_wait(barrier, 5)
        for w in (0, 1):
            start(core_copy(w, j))
    for copy in loads[4:]:
        copy.wait()
    for j in order:
        for w in (0, 1):
            make_state(w, 1, j)

    for n, j in enumerate(order):
        for w in (0, 1):
            core_copy(w, j).wait_recv()
            chip[w, j] = state[w, 1, j] + core_in[w, j]
            if n < 2:
                start(side_copy(w, n, j))

    causal = lax.broadcasted_iota(jnp.int32, (tile, tile), 0) >= lax.broadcasted_iota(jnp.int32, (tile, tile), 1)

    def local(slot):
        @pl.loop(0, COLS)
        def _(j):
            q, k, v, g = (inb[i, slot, j] for i in range(4))
            scores = jnp.where(causal, dot(g, v, NT), 0.0).astype(BF16)
            part[0, slot, j] = dot(scores, k, NN)
            part[1, slot, j] = dot(scores, q, TN)
            scores = jnp.where(causal, dot(q, k, NT), 0.0).astype(BF16)
            part[2, slot, j] = dot(scores, g, TN)

    local(0)
    for w in (0, 1):
        side_copy(w, 0, x).wait_recv()
        far_src[w] = chip[w, COLS - 1 - x] + side_in[w, 0]
        start(far_copy(w))
    local(1)
    for w in (0, 1):
        side_copy(w, 1, x).wait_recv()
        total[w] = chip[w, x] + side_in[w, 1]

    late = lax.div(z, ROWS // 2)
    kinds = [lax.rem(t + late, 2) for t in (0, 1)]
    for w in (0, 1):
        far_copy(w).wait_recv()

    def flag(value):
        return value.astype(F32)

    for w in kinds:
        at = z + w * (ROWS - 1 - 2 * z)
        own_base = flag(right + w * (1 - 2 * right))
        far_base = 1.0 - own_base
        side_self = flag(odd + w * (1 - 2 * odd))
        side_other = 1.0 - side_self

        @pl.when(at == 0)
        def _():
            z_in[w] = jnp.zeros((width, width), F32)

        for k in range(CHUNKS):
            span = part_of(k)

            @pl.when(at > 0)
            def _():
                z_copy(w, k).wait_recv()

            before = z_in[w, span]
            ours = total[w, span]
            theirs = far_in[w, span]

            @pl.when(at < ROWS - 1)
            def _():
                z_src[w, span] = before + (ours + theirs)
                z_copy(w, k).start()

            far_out_src[w, span] = before + far_base * ours
            start(far_back(w, k))
            base = before + own_base * theirs
            side_out_src[w, 1, span] = base + side_other * chip[w, x, span]
            side_out[w, 2, span] = base + side_self * side_in[w, 1, span]
        start(side_back(w, 1))

    core_other = [flag(c + w * (1 - 2 * c)) for w in (0, 1)]

    def hand_over(w, j, offset):
        partner = 1.0 - flag(c + w * (1 - 2 * c))
        core_out_src[w, j] = offset + partner * state[w, 1, j]
        start(core_back(w, j))
        core_out[w, COLS + j] = offset + (1.0 - partner) * core_in[w, j]

    for w in kinds:
        for k in range(CHUNKS):
            far_back(w, k).wait_recv()
        side_self = flag(odd + w * (1 - 2 * odd))
        base = far_out[w]
        side_out_src[w, 0] = base + (1.0 - side_self) * chip[w, COLS - 1 - x]
        start(side_back(w, 0))
        side_out[w, 3] = base + side_self * side_in[w, 0]
        hand_over(w, x, side_out[w, 2])
        hand_over(w, COLS - 1 - x, side_out[w, 3])
    for w in kinds:
        for n, j in ((1, xa), (0, COLS - 1 - xa)):
            side_back(w, n).wait_recv()
            hand_over(w, j, side_out[w, n])

    def finish(slot, parity, j, earlier, later):
        earlier, later = earlier.astype(BF16), later.astype(BF16)
        outb[0, slot, j] = (part[0, slot, j] + dot(inb[3, slot, j], earlier, NT)).astype(BF16)
        outb[1, slot, j] = (part[1, slot, j] + dot(inb[2, slot, j], later, NT)).astype(BF16)
        outb[2, slot, j] = (part[2, slot, j] + dot(inb[1, slot, j], later, NN)).astype(BF16)
        for i, target in enumerate((gq_hbm, gk_hbm, gv_hbm)):
            pltpu.make_async_copy(outb.at[i, slot, j], target.at[j, parity], out_sem.at[i, slot, j]).start()

    order = (x, COLS - 1 - x, xa, COLS - 1 - xa)
    for j in order:
        finish(1, c, j, core_out[0, COLS + j], core_out[1, COLS + j])
    for j in order:
        for w in (0, 1):
            core_back(w, j).wait_recv()
        finish(0, o, j, core_out[0, j], core_out[1, j])

    for copy in sends:
        copy.wait_send()
    for w in kinds:
        at = z + w * (ROWS - 1 - 2 * z)

        @pl.when(at < ROWS - 1)
        def _():
            for k in range(CHUNKS):
                z_copy(w, k).wait_send()

    for slot, parity in ((1, c), (0, o)):
        for j in range(COLS):
            for i, target in enumerate((gq_hbm, gk_hbm, gv_hbm)):
                pltpu.make_async_copy(outb.at[i, slot, j], target.at[j, parity], out_sem.at[i, slot, j]).wait()


def body(queries, key_rows, value_rows, grad_out):
    heads, tile, width = queries.shape
    split = (heads // 2, 2, tile, width)
    square = (width, width)
    sem = pltpu.SemaphoreType.DMA
    half = heads // 2
    grads = pl.pallas_call(
        kernel,
        out_shape=[jax.ShapeDtypeStruct(split, BF16)] * 3,
        in_specs=[pl.BlockSpec(memory_space=pl.ANY)] * 4,
        out_specs=[pl.BlockSpec(memory_space=pl.ANY)] * 3,
        scratch_shapes=[
            pltpu.VMEM((4, 2, half, tile, width), BF16),
            pltpu.VMEM((3, 2, half, tile, width), F32),
            pltpu.VMEM((3, 2, half, tile, width), BF16),
            pltpu.VMEM((2, 2, half, *square), F32),
            pltpu.VMEM((2, half, *square), F32),
            pltpu.VMEM((2, half, *square), F32),
            pltpu.VMEM((2, 2, *square), F32),
            pltpu.VMEM((2, *square), F32),
            pltpu.VMEM((2, *square), F32),
            pltpu.VMEM((2, *square), F32),
            pltpu.VMEM((2, *square), F32),
            pltpu.VMEM((2, *square), F32),
            pltpu.VMEM((2, *square), F32),
            pltpu.VMEM((2, *square), F32),
            pltpu.VMEM((2, 2, *square), F32),
            pltpu.VMEM((2, 4, *square), F32),
            pltpu.VMEM((2, half, *square), F32),
            pltpu.VMEM((2, 2 * half, *square), F32),
            sem((4, 2)),
            sem((3, 2, half)),
            sem((2, half)), sem((2, half)),
            sem((2, 2)), sem((2, 2)),
            sem((2,)), sem((2,)),
            sem((2, CHUNKS)), sem((2, CHUNKS)),
            sem((2, CHUNKS)), sem((2, CHUNKS)),
            sem((2, 2)), sem((2, 2)),
            sem((2, half)), sem((2, half)),
        ],
        compiler_params=pltpu.CompilerParams(
            collective_id=0, has_side_effects=True, vmem_limit_bytes=48 * 2**20
        ),
    )(*(a.reshape(split) for a in (queries, key_rows, value_rows, grad_out)))
    return tuple(g.reshape(heads, tile, width) for g in grads)


def solution(mesh):
    placed = P("head", "seq", None)
    return jax.shard_map(
        body, mesh=mesh, in_specs=(placed,) * 4, out_specs=(placed,) * 3, check_vma=False
    )
```

```python
import jax
import jax.numpy as jnp
from jax import lax
from jax.experimental import pallas as pl
from jax.experimental.pallas import tpu as pltpu
from jax.sharding import PartitionSpec as P

ROWS, COLS, PER = 8, 4, 2
HALF = ROWS // 2
F32, BF16 = jnp.float32, jnp.bfloat16
NN = (((1,), (0,)), ((), ()))
NT = (((1,), (1,)), ((), ()))
TN = (((0,), (0,)), ((), ()))


def dot(a, b, dims):
    return lax.dot_general(a, b, dims, preferred_element_type=F32)


def kernel(
    k_hbm, v_hbm, q_hbm, g_hbm,
    gq, gk, gv,
    inb, part, own, away, core_in, chip, row_in, ahead, rowsum, col_in, offset, half_src, half_in,
    row_src, row_out, core_src, core_out,
    in_sem,
    ci_s, ci_r, ri_s, ri_r, z_s, z_r, h_s, h_r, ro_s, ro_r, co_s, co_r, ready,
):
    tile, width = inb.shape[3:]
    place = lax.axis_index("seq")
    c = lax.rem(place, 2)
    x = lax.rem(lax.div(place, 2), COLS)
    z = lax.div(place, 2 * COLS)
    px = x + c * (COLS - 1 - 2 * x)
    p = z + c * (ROWS - 1 - 2 * z)
    g = lax.div(p, HALF)
    i = lax.rem(p, HALF)

    def device(pp, ppx):
        zz = pp + c * (ROWS - 1 - 2 * pp)
        xx = ppx + c * (COLS - 1 - 2 * ppx)
        return {"seq": (zz * COLS + xx) * 2 + c}

    partner = {"seq": place + 1 - 2 * c}

    def row_place(start, off):
        return lax.rem(start + off, COLS)

    loads = []
    for a, source in ((2, q_hbm), (3, g_hbm), (0, k_hbm), (1, v_hbm)):
        for n in range(2):
            span = pl.ds(n * 2, 2)
            copy = pltpu.make_async_copy(source.at[span], inb.at[a, span], in_sem.at[a, n])
            copy.start()
            loads.append(copy)

    barrier = pltpu.get_barrier_semaphore()

    def greet(peer):
        pl.semaphore_signal(barrier, inc=1, device_id=peer, device_id_type=pl.DeviceIdType.MESH)

    greet(partner)
    for off in (1, 2, 3):
        greet(device(p, row_place(px, off)))
    first = lax.rem(z, HALF)
    for d in range(HALF):
        @pl.when(d > first)
        def _():
            zz = z - first + d
            greet({"seq": (zz * COLS + x) * 2 + c})

    for low, high, core in ((0, 7, 0), (0, 6, 0), (3, 4, 0), (3, 5, 0), (0, 7, 1), (1, 7, 1), (3, 4, 1), (2, 4, 1)):
        @pl.when((z == low) & (c == core))
        def _():
            greet({"seq": (high * COLS + x) * 2 + core})

    upper = lax.div(z, HALF)
    ends = jnp.where((z == 7) | (z == 4), 2, 0)
    expected = 4 + first + jnp.where(c == 0, upper, ends)

    def remote(src, dst, send, recv, peer):
        return pltpu.make_async_remote_copy(
            src_ref=src, dst_ref=dst, send_sem=send, recv_sem=recv, device_id=peer,
            device_id_type=pl.DeviceIdType.MESH,
        )

    sends = []

    def start(copy):
        copy.start()
        sends.append(copy)

    def core_copy(j, u):
        return remote(away.at[j, u], core_in.at[j, u], ci_s.at[j, u], ci_r.at[j, u], partner)

    def row_copy(off, u):
        j = row_place(px, off)
        return remote(chip.at[j, u], row_in.at[px, u], ri_s.at[off, u], ri_r.at[px, u], device(p, j))

    def col_copy(d, u):
        return remote(rowsum.at[u], col_in.at[i, u], z_s.at[d, u], z_r.at[i, u], device(g * HALF + d, px))

    def half_copy(to, n, u):
        return remote(half_src.at[u], half_in.at[u], h_s.at[n, u], h_r.at[u], device(to, px))

    def row_back(off, u):
        j = row_place(px, off)
        return remote(row_src.at[off, u], row_out.at[px, u], ro_s.at[off, u], ro_r.at[px, u], device(p, j))

    def core_back(j, u):
        return remote(core_src.at[j, u], core_out.at[j, u], co_s.at[j, u], co_r.at[j, u], partner)

    def arrival(ref, sem):
        return remote(ref, ref, sem, sem, partner)

    other_px = COLS - 1 - px
    for copy in loads:
        copy.wait()
    for u in range(PER):
        for off in (2, 1, 3, 0):
            j = row_place(other_px, off)
            kind = 2 * (1 - c)
            away[j, u] = dot(inb[kind, j, u], inb[kind + 1, j, u], TN)
            if u == 0 and off == 2:
                pl.semaphore_wait(barrier, expected)
            start(core_copy(j, u))

    def answer(sender):
        pl.semaphore_signal(
            ready.at[p], inc=1, device_id=device(sender, px), device_id_type=pl.DeviceIdType.MESH
        )

    for s in range(HALF):
        @pl.when((c == 0) & (s < i))
        def _():
            answer(g * HALF + s)

        @pl.when((c == 1) & (p == 0) & (s > 0))
        def _():
            answer(s)

    @pl.when((c == 0) & (g == 1))
    def _():
        answer(jnp.where(i < 2, HALF - 1, 0))

    for u in range(PER):
        for off in (2, 1, 3, 0):
            j = row_place(px, off)
            own[j, u] = dot(inb[2 * c, j, u], inb[2 * c + 1, j, u], TN)

    for u in range(PER):
        for off in (2, 1, 3, 0):
            j = row_place(px, off)
            core_copy(j, u).wait_recv()
            if off:
                chip[j, u] = own[j, u] + core_in[j, u]
                start(row_copy(off, u))
            else:
                row_in[px, u] = own[px, u] + core_in[px, u]

    causal = lax.broadcasted_iota(jnp.int32, (tile, tile), 0) >= lax.broadcasted_iota(jnp.int32, (tile, tile), 1)

    def local(half):
        @pl.loop(0, COLS)
        def _(n):
            j, u = half * 2 + lax.div(n, 2), lax.rem(n, 2)
            k, v, q, go = (inb[a, j, u] for a in range(4))
            scores = jnp.where(causal, dot(go, v, NT), 0.0).astype(BF16)
            part[0, j, u] = dot(scores, k, NN)
            part[1, j, u] = dot(scores, q, TN)
            scores = jnp.where(causal, dot(q, k, NT), 0.0).astype(BF16)
            part[2, j, u] = dot(scores, go, TN)

    local(0)
    lower_end = (g == 0) & ((i == 0) | (i == HALF - 1))

    for u in range(PER):
        for off in (1, 3, 2):
            j = row_place(px, off)
            arrival(row_in.at[j, u], ri_r.at[j, u]).wait_recv()
        total = row_in[0, u]
        ahead[0, u] = jnp.zeros((width, width), F32)
        ahead[1, u] = total
        total = total + row_in[1, u]
        ahead[2, u] = total
        total = total + row_in[2, u]
        ahead[3, u] = total
        rowsum[u] = total + row_in[3, u]
        for d in range(HALF):
            @pl.when((d > i) | ((g == 0) & (i > 0) & (d == 0)))
            def _():
                if u == 0:
                    @pl.when((c == 0) == (d > i))
                    def _():
                        pl.semaphore_wait(ready.at[g * HALF + d], 1)
                col_copy(d, u).start()

    @pl.when(g == 1)
    def _():
        local(1)

    for u in range(PER):
        offset[u] = jnp.zeros((width, width), F32)
        for s in range(HALF - 1):
            @pl.when(s < i)
            def _():
                arrival(col_in.at[s, u], z_r.at[s, u]).wait_recv()
                offset[u] += col_in[s, u]

        for end, targets in ((0, (7, 6)), (HALF - 1, (4, 5))):
            @pl.when((g == 0) & (i == end))
            def _():
                if end == 0:
                    for s in range(1, HALF):
                        arrival(col_in.at[s, u], z_r.at[s, u]).wait_recv()
                    half_src[u] = rowsum[u] + col_in[1, u] + col_in[2, u] + col_in[3, u]
                else:
                    half_src[u] = offset[u] + rowsum[u]
                for n, to in enumerate(targets):
                    if u == 0:
                        @pl.when(c == 0)
                        def _():
                            pl.semaphore_wait(ready.at[to], 1)
                    half_copy(to, n, u).start()

        @pl.when(g == 1)
        def _():
            arrival(half_in.at[u], h_r.at[u]).wait_recv()
            offset[u] += half_in[u]

        for off in (2, 1, 3):
            row_src[off, u] = offset[u] + ahead[row_place(px, off), u]
            start(row_back(off, u))
        row_out[px, u] = offset[u] + ahead[px, u]

    @pl.when(g == 0)
    def _():
        local(1)

    def emit(n, j, u, value):
        (gq, gk, gv)[n][j, u] = (part[n, j, u] + value).astype(BF16)

    def finish(kind, j, u, state):
        state = state.astype(BF16)

        @pl.when(kind == 0)
        def _():
            emit(0, j, u, dot(inb[3, j, u], state, NT))

        @pl.when(kind == 1)
        def _():
            emit(1, j, u, dot(inb[1, j, u], state, NT))
            emit(2, j, u, dot(inb[0, j, u], state, NN))

    def turn(n):
        m = lax.rem(n, COLS)
        return m + lax.div(m, 2) * (1 - 2 * lax.rem(m, 2)), lax.div(n, COLS)

    def own_kind():
        @pl.loop(0, COLS * PER)
        def _(n):
            off, u = turn(n)
            j = row_place(px, off)

            @pl.when(off > 0)
            def _():
                arrival(row_out.at[j, u], ro_r.at[j, u]).wait_recv()

            core_src[j, u] = row_out[j, u] + own[j, u]
            core_back(j, u).start()
            finish(c, j, u, row_out[j, u])

    def other_kind():
        @pl.loop(0, COLS * PER)
        def _(n):
            off, u = turn(n)
            j = row_place(other_px, off)
            core_back(j, u).wait_recv()
            finish(1 - c, j, u, core_out[j, u])

    @pl.when(g == 1)
    def _():
        other_kind()

    own_kind()

    @pl.when(g == 0)
    def _():
        other_kind()

    for copy in sends:
        copy.wait_send()
    for u in range(PER):
        for d in range(HALF):
            @pl.when((d > i) | ((g == 0) & (i > 0) & (d == 0)))
            def _():
                col_copy(d, u).wait_send()

        @pl.when(lower_end)
        def _():
            for n in range(2):
                half_copy(0, n, u).wait_send()

        for j in range(COLS):
            core_back(j, u).wait_send()


def put(*refs):
    sources, targets, sems = refs[:3], refs[3:6], refs[6]
    copies = [
        pltpu.make_async_copy(sources[n].at[j], targets[n].at[j], sems.at[n, j])
        for n in range(3)
        for j in range(COLS)
    ]
    for copy in copies:
        copy.start()
    for copy in copies:
        copy.wait()


def body(queries, key_rows, value_rows, grad_out):
    heads, tile, width = queries.shape
    split = (COLS, PER, tile, width)
    square = (width, width)
    sem = pltpu.SemaphoreType.DMA
    four = pltpu.VMEM((COLS, PER, *square), F32)
    two = pltpu.VMEM((PER, *square), F32)
    pairs = sem((COLS, PER))
    grads = pl.pallas_call(
        kernel,
        out_shape=[pltpu.VMEM(split, BF16)] * 3,
        in_specs=[pl.BlockSpec(memory_space=pl.ANY)] * 4,
        out_specs=[pl.BlockSpec(memory_space=pltpu.VMEM)] * 3,
        scratch_shapes=[
            pltpu.VMEM((4, *split), BF16),
            pltpu.VMEM((3, *split), F32),
            four, four, four, four, four, four, two, four, two, two, two,
            four, four, four, four,
            sem((4, 2)),
            pairs, pairs, pairs, pairs, pairs, pairs, sem((2, PER)), sem((PER,)), pairs, pairs, pairs, pairs,
            pltpu.SemaphoreType.REGULAR((ROWS,)),
        ],
        compiler_params=pltpu.CompilerParams(
            collective_id=0, has_side_effects=True, vmem_limit_bytes=61 * 2**20
        ),
    )(*(a.reshape(split) for a in (key_rows, value_rows, queries, grad_out)))
    grads = pl.pallas_call(
        put,
        out_shape=[jax.ShapeDtypeStruct(split, BF16)] * 3,
        in_specs=[pl.BlockSpec(memory_space=pl.ANY)] * 3,
        out_specs=[pl.BlockSpec(memory_space=pl.ANY)] * 3,
        scratch_shapes=[sem((3, COLS))],
        compiler_params=pltpu.CompilerParams(vmem_limit_bytes=2**20),
    )(*grads)
    return tuple(a.reshape(heads, tile, width) for a in grads)


def solution(mesh):
    placed = P("head", "seq", None)
    return jax.shard_map(
        body, mesh=mesh, in_specs=(placed,) * 4, out_specs=(placed,) * 3, check_vma=False
    )
```

```python
import jax
import jax.numpy as jnp
from jax import lax
from jax.experimental import pallas as pl
from jax.experimental.pallas import tpu as pltpu
from jax.sharding import PartitionSpec as P

ROWS, COLS, PER = 8, 4, 2
HALF = ROWS // 2
F32, BF16 = jnp.float32, jnp.bfloat16
NN = (((1,), (0,)), ((), ()))
NT = (((1,), (1,)), ((), ()))
TN = (((0,), (0,)), ((), ()))


def dot(a, b, dims):
    return lax.dot_general(a, b, dims, preferred_element_type=F32)


def kernel(
    k_hbm, v_hbm, q_hbm, g_hbm,
    gq, gk, gv,
    inb, part, own, away, core_in, chip, row_in, ahead, rowsum, col_in, offset, half_src, half_in, pair_src,
    row_src, row_out, core_src, core_out,
    in_sem,
    ci_s, ci_r, ri_s, ri_r, z_s, z_r, h_s, h_r, ro_s, ro_r, co_s, co_r, ready, row_ready,
):
    tile, width = inb.shape[3:]
    place = lax.axis_index("seq")
    c = lax.rem(place, 2)
    x = lax.rem(lax.div(place, 2), COLS)
    z = lax.div(place, 2 * COLS)
    px = x + c * (COLS - 1 - 2 * x)
    p = z + c * (ROWS - 1 - 2 * z)
    g = lax.div(p, HALF)
    i = lax.rem(p, HALF)

    def device(pp, ppx):
        zz = pp + c * (ROWS - 1 - 2 * pp)
        xx = ppx + c * (COLS - 1 - 2 * ppx)
        return {"seq": (zz * COLS + xx) * 2 + c}

    partner = {"seq": place + 1 - 2 * c}

    def row_place(start, off):
        return lax.rem(start + off, COLS)

    barrier = pltpu.get_barrier_semaphore()

    def greet(peer):
        pl.semaphore_signal(barrier, inc=1, device_id=peer, device_id_type=pl.DeviceIdType.MESH)

    greet(partner)
    for off in (1, 2, 3):
        greet({"seq": (z * COLS + row_place(x, off)) * 2 + 1})
    first = lax.rem(z, HALF)
    for d in range(HALF):
        @pl.when(d > first)
        def _():
            zz = z - first + d
            greet({"seq": (zz * COLS + x) * 2 + c})

    for low, high, core in ((0, 7, 0), (0, 6, 0), (3, 4, 0), (3, 5, 0), (0, 7, 1), (1, 7, 1), (3, 4, 1), (2, 4, 1), (3, 6, 0), (1, 4, 1)):
        @pl.when((z == low) & (c == core))
        def _():
            greet({"seq": (high * COLS + x) * 2 + core})

    sources = (k_hbm, v_hbm, q_hbm, g_hbm)
    other_px = COLS - 1 - px

    def load(source, a, j, u):
        return pltpu.make_async_copy(source.at[j, u], inb.at[a, j, u], in_sem.at[a, j, u])

    for core in range(2):
        @pl.when(c == core)
        def _():
            for kind, begin in ((1 - core, other_px), (core, px)):
                for u in range(PER):
                    for off in (2, 1, 3, 0):
                        for a in (2 * kind, 2 * kind + 1):
                            load(sources[a], a, row_place(begin, off), u).start()

    upper = lax.div(z, HALF)
    late_end = jnp.where(z == 7, 2, 0) + jnp.where(z == 4, 3, 0)
    column = upper + jnp.where(z == 6, 1, 0)
    expected = 1 + first + jnp.where(c == 0, column, 6 + late_end)

    def remote(src, dst, send, recv, peer):
        return pltpu.make_async_remote_copy(
            src_ref=src, dst_ref=dst, send_sem=send, recv_sem=recv, device_id=peer,
            device_id_type=pl.DeviceIdType.MESH,
        )

    def core_copy(j, u):
        return remote(away.at[j, u], core_in.at[j, u], ci_s.at[j, u], ci_r.at[j, u], partner)

    def row_copy(off, u):
        j = row_place(px, off)
        return remote(chip.at[j, u], row_in.at[px, u], ri_s.at[off, u], ri_r.at[px, u], device(p, j))

    def pair_copy(d, u):
        return remote(pair_src.at[u], col_in.at[1, u], z_s.at[d, u], z_r.at[1, u], device(g * HALF + d, px))

    def col_copy(d, u):
        return remote(rowsum.at[u], col_in.at[i, u], z_s.at[d, u], z_r.at[i, u], device(g * HALF + d, px))

    def half_copy(to, n, u):
        return remote(half_src.at[u], half_in.at[u], h_s.at[n, u], h_r.at[u], device(to, px))

    def row_back(off, u):
        j = row_place(px, off)
        return remote(row_src.at[off, u], row_out.at[px, u], ro_s.at[off, u], ro_r.at[px, u], device(p, j))

    def core_back(j, u):
        return remote(core_src.at[j, u], core_out.at[j, u], co_s.at[j, u], co_r.at[j, u], partner)

    def arrival(ref, sem):
        return remote(ref, ref, sem, sem, partner)

    def states(kind, begin, into):
        places = [(row_place(begin, off), u) for u in range(PER) for off in (2, 1, 3, 0)]
        for j, u in places:
            for a in (2 * kind, 2 * kind + 1):
                load(k_hbm, a, j, u).wait()
        for j, u in places:
            into[j, u] = dot(inb[2 * kind, j, u], inb[2 * kind + 1, j, u], TN)

    states(1 - c, other_px, away)
    pl.semaphore_wait(barrier, expected)
    for u in range(PER):
        for off in (2, 1, 3, 0):
            core_copy(row_place(other_px, off), u).start()

    @pl.when(c == 1)
    def _():
        pl.semaphore_signal(row_ready, inc=1, device_id=partner, device_id_type=pl.DeviceIdType.MESH)

    states(c, px, own)

    def answer(sender):
        pl.semaphore_signal(
            ready.at[p], inc=1, device_id=device(sender, px), device_id_type=pl.DeviceIdType.MESH
        )

    for s in range(HALF):
        @pl.when((c == 0) & (g == 0) & (s < i))
        def _():
            answer(s)

        @pl.when((c == 1) & (p == 0) & (s > 0))
        def _():
            answer(s)

    @pl.when((c == 0) & (g == 1))
    def _():
        answer(jnp.where(i < 2, HALF - 1, 0))

    @pl.when((c == 0) & (p == 6))
    def _():
        answer(HALF - 1)

    for src, d in ((0, 1), (1, 2), (1, 3), (2, 3)):
        @pl.when((c == 0) & (g == 1) & (i == d))
        def _():
            answer(HALF + src)

    causal = lax.broadcasted_iota(jnp.int32, (tile, tile), 0) >= lax.broadcasted_iota(jnp.int32, (tile, tile), 1)

    def local(half):
        @pl.loop(0, COLS)
        def _(n):
            j, u = half * 2 + lax.div(n, 2), lax.rem(n, 2)
            k, v, q, go = (inb[a, j, u] for a in range(4))
            scores = jnp.where(causal, dot(go, v, NT), 0.0).astype(BF16)
            part[0, j, u] = dot(scores, k, NN)
            part[1, j, u] = dot(scores, q, TN)
            scores = jnp.where(causal, dot(q, k, NT), 0.0).astype(BF16)
            part[2, j, u] = dot(scores, go, TN)

    @pl.when((c == 0) & (g == 1))
    def _():
        local(0)
        local(1)

    @pl.when(c == 0)
    def _():
        pl.semaphore_wait(row_ready, 1)

    for u in range(PER):
        for off in (2, 1, 3, 0):
            j = row_place(px, off)
            core_copy(j, u).wait_recv()
            if off:
                chip[j, u] = own[j, u] + core_in[j, u]
                row_copy(off, u).start()
            else:
                row_in[px, u] = own[px, u] + core_in[px, u]

    def ready_for(d):
        @pl.when((c == 0) == (d > i))
        def _():
            pl.semaphore_wait(ready.at[g * HALF + d], 1)

    def send_column(u, targets):
        for d in targets:
            @pl.when((g == 0) & ((d > i) | ((i > 0) & (d == 0))))
            def _():
                if u == 0:
                    ready_for(d)
                col_copy(d, u).start()

        for src, d in ((0, 1), (2, 3)) if 0 in targets else ():
            @pl.when((g == 1) & (i == src))
            def _():
                if u == 0:
                    ready_for(d)
                col_copy(d, u).start()

    @pl.when((c == 1) | (g == 0))
    def _():
        local(0)

    for u in range(PER):
        for off in (1, 3, 2):
            j = row_place(px, off)
            arrival(row_in.at[j, u], ri_r.at[j, u]).wait_recv()
        total = row_in[0, u]
        ahead[0, u] = jnp.zeros((width, width), F32)
        ahead[1, u] = total
        total = total + row_in[1, u]
        ahead[2, u] = total
        total = total + row_in[2, u]
        ahead[3, u] = total
        rowsum[u] = total + row_in[3, u]

        send_column(u, (0, 3))

    for u in range(PER):
        send_column(u, (2, 1))

    @pl.when((c == 1) & (g == 1))
    def _():
        local(1)


    def row_result(u):
        for off in (2, 1, 3):
            row_src[off, u] = offset[u] + ahead[row_place(px, off), u]
            row_back(off, u).start()
        row_out[px, u] = offset[u] + ahead[px, u]

    def takes(s):
        terms = (i == 1) if s == 0 else (i > 1) if s == 1 else (i == 3)
        return ((g == 0) & (s < i)) | ((g == 1) & terms)

    for u in range(PER):
        offset[u] = jnp.zeros((width, width), F32)
        for s in range(HALF - 1):
            @pl.when(takes(s))
            def _():
                arrival(col_in.at[s, u], z_r.at[s, u]).wait_recv()
                offset[u] += col_in[s, u]

        @pl.when((g == 1) & (i == 1))
        def _():
            pair_src[u] = offset[u] + rowsum[u]
            for d in (3, 2):
                if u == 0:
                    ready_for(d)
                pair_copy(d, u).start()

        @pl.when((g == 0) & (c == 0))
        def _():
            row_result(u)

    for u in range(PER):
        for end, targets in ((0, (7, 6, None)[: 2 - u]), (HALF - 1, (None, 6, 5, 4)[2 - u :])):
            @pl.when((g == 0) & (i == end))
            def _():
                if end == 0:
                    for s in range(1, HALF):
                        arrival(col_in.at[s, u], z_r.at[s, u]).wait_recv()
                    half_src[u] = rowsum[u] + col_in[1, u] + col_in[2, u] + col_in[3, u]
                else:
                    half_src[u] = offset[u] + rowsum[u]
                for n, to in enumerate(targets):
                    if u == 0 or to == 6:
                        @pl.when(c == 0)
                        def _():
                            pl.semaphore_wait(ready.at[to], 1)
                    half_copy(to, n, u).start()

    for u in range(PER):
        @pl.when(g == 1)
        def _():
            arrival(half_in.at[u], h_r.at[u]).wait_recv()
            offset[u] += half_in[u]

        @pl.when((g == 1) | (c == 1))
        def _():
            row_result(u)

    @pl.when(g == 0)
    def _():
        local(1)

    def emit(n, j, u, value):
        (gq, gk, gv)[n][j, u] = (part[n, j, u] + value).astype(BF16)

    def finish(kind, places, states_in):
        @pl.when(kind == 0)
        def _():
            for j, u in places:
                emit(0, j, u, dot(inb[3, j, u], states_in[j, u].astype(BF16), NT))

        @pl.when(kind == 1)
        def _():
            for j, u in places:
                state = states_in[j, u].astype(BF16)
                emit(1, j, u, dot(inb[1, j, u], state, NT))
                emit(2, j, u, dot(inb[0, j, u], state, NN))

    def own_kind():
        for u in range(PER):
            places = [(row_place(px, off), u) for off in (0, 1, 3, 2)]
            for n, (j, _) in enumerate(places):
                if n:
                    arrival(row_out.at[j, u], ro_r.at[j, u]).wait_recv()
                core_src[j, u] = row_out[j, u] + own[j, u]
                core_back(j, u).start()
            finish(c, places, row_out)

    def other_kind():
        for u in range(PER):
            places = [(row_place(other_px, off), u) for off in (0, 1, 3, 2)]
            for batch in (places,) if u == 0 else (places[:3], places[3:]):
                for j, _ in batch:
                    core_back(j, u).wait_recv()
                finish(1 - c, batch, core_out)

    @pl.when(g == 1)
    def _():
        other_kind()

    own_kind()

    @pl.when(g == 0)
    def _():
        other_kind()

    for u in range(PER):
        for off in (1, 2, 3):
            row_copy(off, u).wait_send()
            row_back(off, u).wait_send()
        for d in range(HALF):
            back = (i > 0) if d == 0 else (i == 0) if d == 1 else (i == 1) if d == 2 else (i == 1) | (i == 2)
            forward = (d > i) | ((i > 0) & (d == 0))
            @pl.when(((g == 0) & forward) | ((g == 1) & back & (d > 0)))
            def _():
                col_copy(d, u).wait_send()

        for end, count in ((0, 2 - u), (HALF - 1, 2 + u)):
            @pl.when((g == 0) & (i == end))
            def _():
                for n in range(count):
                    half_copy(0, n, u).wait_send()

        for j in range(COLS):
            core_copy(j, u).wait_send()
            core_back(j, u).wait_send()


def put(*refs):
    sources, targets, sems = refs[:3], refs[3:6], refs[6]
    copies = [
        pltpu.make_async_copy(sources[n].at[j], targets[n].at[j], sems.at[n, j])
        for n in range(3)
        for j in range(COLS)
    ]
    for copy in copies:
        copy.start()
    for copy in copies:
        copy.wait()


def body(queries, key_rows, value_rows, grad_out):
    heads, tile, width = queries.shape
    split = (COLS, PER, tile, width)
    square = (width, width)
    sem = pltpu.SemaphoreType.DMA
    four = pltpu.VMEM((COLS, PER, *square), F32)
    two = pltpu.VMEM((PER, *square), F32)
    pairs = sem((COLS, PER))
    grads = pl.pallas_call(
        kernel,
        out_shape=[pltpu.VMEM(split, BF16)] * 3,
        in_specs=[pl.BlockSpec(memory_space=pl.ANY)] * 4,
        out_specs=[pl.BlockSpec(memory_space=pltpu.VMEM)] * 3,
        scratch_shapes=[
            pltpu.VMEM((4, *split), BF16),
            pltpu.VMEM((3, *split), F32),
            four, four, four, four, four, four, two, four, two, two, two, two,
            four, four, four, four,
            sem((4, COLS, PER)),
            pairs, pairs, pairs, pairs, pairs, pairs, sem((3, PER)), sem((PER,)), pairs, pairs, pairs, pairs,
            pltpu.SemaphoreType.REGULAR((ROWS,)),
            pltpu.SemaphoreType.REGULAR,
        ],
        compiler_params=pltpu.CompilerParams(
            collective_id=0, has_side_effects=True, vmem_limit_bytes=61 * 2**20
        ),
    )(*(a.reshape(split) for a in (key_rows, value_rows, queries, grad_out)))
    grads = pl.pallas_call(
        put,
        out_shape=[jax.ShapeDtypeStruct(split, BF16)] * 3,
        in_specs=[pl.BlockSpec(memory_space=pl.ANY)] * 3,
        out_specs=[pl.BlockSpec(memory_space=pl.ANY)] * 3,
        scratch_shapes=[sem((3, COLS))],
        compiler_params=pltpu.CompilerParams(vmem_limit_bytes=2**20),
    )(*grads)
    return tuple(a.reshape(heads, tile, width) for a in grads)


def solution(mesh):
    placed = P("head", "seq", None)
    return jax.shard_map(
        body, mesh=mesh, in_specs=(placed,) * 4, out_specs=(placed,) * 3, check_vma=False
    )
```

```python
import jax
import jax.numpy as jnp
from jax import lax
from jax.experimental import pallas as pl
from jax.experimental.pallas import tpu as pltpu
from jax.sharding import PartitionSpec as P

ROWS, COLS, PER = 8, 4, 2
HALF = ROWS // 2
F32, BF16 = jnp.float32, jnp.bfloat16
NN = (((1,), (0,)), ((), ()))
NT = (((1,), (1,)), ((), ()))
TN = (((0,), (0,)), ((), ()))


def dot(a, b, dims):
    return lax.dot_general(a, b, dims, preferred_element_type=F32)


def kernel(
    k_hbm, v_hbm, q_hbm, g_hbm,
    gq, gk, gv,
    inb, part, own, away, core_in, chip, row_in, ahead, rowsum, col_in, offset, half_src, half_in, pair_src,
    row_src, row_out, core_src, core_out,
    in_sem,
    ci_s, ci_r, ri_s, ri_r, z_s, z_r, h_s, h_r, ro_s, ro_r, co_s, co_r, ready, row_ready,
):
    tile, width = inb.shape[3:]
    place = lax.axis_index("seq")
    c = lax.rem(place, 2)
    x = lax.rem(lax.div(place, 2), COLS)
    z = lax.div(place, 2 * COLS)
    px = x + c * (COLS - 1 - 2 * x)
    p = z + c * (ROWS - 1 - 2 * z)
    g = lax.div(p, HALF)
    i = lax.rem(p, HALF)

    def device(pp, ppx):
        zz = pp + c * (ROWS - 1 - 2 * pp)
        xx = ppx + c * (COLS - 1 - 2 * ppx)
        return {"seq": (zz * COLS + xx) * 2 + c}

    partner = {"seq": place + 1 - 2 * c}

    def row_place(start, off):
        return lax.rem(start + off, COLS)

    barrier = pltpu.get_barrier_semaphore()

    def greet(peer):
        pl.semaphore_signal(barrier, inc=1, device_id=peer, device_id_type=pl.DeviceIdType.MESH)

    greet(partner)
    for off in (1, 2, 3):
        greet({"seq": (z * COLS + row_place(x, off)) * 2 + 1})
    first = lax.rem(z, HALF)
    for d in range(HALF):
        @pl.when(d > first)
        def _():
            zz = z - first + d
            greet({"seq": (zz * COLS + x) * 2 + c})

    for low, high, core in ((0, 7, 0), (0, 6, 0), (3, 4, 0), (3, 5, 0), (0, 7, 1), (1, 7, 1), (3, 4, 1), (2, 4, 1), (3, 6, 0), (1, 4, 1)):
        @pl.when((z == low) & (c == core))
        def _():
            greet({"seq": (high * COLS + x) * 2 + core})

    sources = (k_hbm, v_hbm, q_hbm, g_hbm)
    other_px = COLS - 1 - px

    def load(source, a):
        return pltpu.make_async_copy(source, inb.at[a], in_sem.at[a])

    for a in (2, 3, 0, 1):
        load(sources[a], a).start()

    upper = lax.div(z, HALF)
    late_end = jnp.where(z == 7, 2, 0) + jnp.where(z == 4, 3, 0)
    column = upper + jnp.where(z == 6, 1, 0)
    expected = 1 + first + jnp.where(c == 0, column, 6 + late_end)

    def remote(src, dst, send, recv, peer):
        return pltpu.make_async_remote_copy(
            src_ref=src, dst_ref=dst, send_sem=send, recv_sem=recv, device_id=peer,
            device_id_type=pl.DeviceIdType.MESH,
        )

    def core_copy(j, u):
        return remote(away.at[j, u], core_in.at[j, u], ci_s, ci_r.at[j, u], partner)

    def row_copy(off, u):
        j = row_place(px, off)
        return remote(chip.at[j, u], row_in.at[px, u], ri_s, ri_r.at[u], device(p, j))

    def pair_copy(d, u):
        return remote(pair_src.at[u], col_in.at[1, u], z_s.at[d], z_r.at[1, u], device(g * HALF + d, px))

    def col_copy(d, u):
        return remote(rowsum.at[u], col_in.at[i, u], z_s.at[d], z_r.at[i, u], device(g * HALF + d, px))

    def half_copy(to, u):
        return remote(half_src.at[u], half_in.at[u], h_s.at[u], h_r.at[u], device(to, px))

    def row_back(off, u):
        j = row_place(px, off)
        return remote(row_src.at[off, u], row_out.at[px, u], ro_s, ro_r.at[px, u], device(p, j))

    def core_back(j, u, off):
        batch = u + 1 if u == 1 and off == 2 else u
        return remote(core_src.at[j, u], core_out.at[j, u], co_s, co_r.at[batch], partner)

    def arrival(ref, sem):
        return remote(ref, ref, sem, sem, partner)

    def states(kind, begin, into):
        places = [(row_place(begin, off), u) for u in range(PER) for off in (2, 1, 3, 0)]
        for a in (2 * kind, 2 * kind + 1):
            load(k_hbm, a).wait()
        for j, u in places:
            into[j, u] = dot(inb[2 * kind, j, u], inb[2 * kind + 1, j, u], TN)

    def hand_in():
        pl.semaphore_wait(barrier, expected)
        for u in range(PER):
            for off in (2, 1, 3, 0):
                core_copy(row_place(other_px, off), u).start()

    @pl.when(c == 0)
    def _():
        states(1, other_px, away)
        hand_in()
        states(0, px, own)

    @pl.when(c == 1)
    def _():
        states(1, px, own)
        states(0, other_px, away)
        hand_in()
        pl.semaphore_signal(row_ready, inc=1, device_id=partner, device_id_type=pl.DeviceIdType.MESH)

    def answer(sender):
        pl.semaphore_signal(
            ready.at[p], inc=1, device_id=device(sender, px), device_id_type=pl.DeviceIdType.MESH
        )

    for s in range(HALF):
        @pl.when((c == 0) & (g == 0) & (s < i))
        def _():
            answer(s)

        @pl.when((c == 1) & (p == 0) & (s > 0))
        def _():
            answer(s)

    @pl.when((c == 0) & (g == 1))
    def _():
        answer(jnp.where(i < 2, HALF - 1, 0))

    @pl.when((c == 0) & (p == 6))
    def _():
        answer(HALF - 1)

    for src, d in ((0, 1), (1, 2), (1, 3), (2, 3)):
        @pl.when((c == 0) & (g == 1) & (i == d))
        def _():
            answer(HALF + src)

    causal = lax.broadcasted_iota(jnp.int32, (tile, tile), 0) >= lax.broadcasted_iota(jnp.int32, (tile, tile), 1)

    def local(half):
        @pl.loop(0, COLS)
        def _(n):
            j, u = half * 2 + lax.div(n, 2), lax.rem(n, 2)
            k, v, q, go = (inb[a, j, u] for a in range(4))
            scores = jnp.where(causal, dot(go, v, NT), 0.0).astype(BF16)
            part[0, j, u] = dot(scores, k, NN)
            part[1, j, u] = dot(scores, q, TN)
            scores = jnp.where(causal, dot(q, k, NT), 0.0).astype(BF16)
            part[2, j, u] = dot(scores, go, TN)

    @pl.when((c == 0) & (g == 1))
    def _():
        local(0)
        local(1)

    @pl.when(c == 0)
    def _():
        pl.semaphore_wait(row_ready, 1)

    for u in range(PER):
        for off in (2, 1, 3, 0):
            j = row_place(px, off)
            core_copy(j, u).wait_recv()
            if off:
                chip[j, u] = own[j, u] + core_in[j, u]
                row_copy(off, u).start()
            else:
                row_in[px, u] = own[px, u] + core_in[px, u]

    def ready_for(d):
        @pl.when((c == 0) == (d > i))
        def _():
            pl.semaphore_wait(ready.at[g * HALF + d], 1)

    def send_column(u, targets):
        for d in targets:
            @pl.when((g == 0) & ((d > i) | ((i > 0) & (d == 0))))
            def _():
                if u == 0:
                    ready_for(d)
                col_copy(d, u).start()

        for src, d in ((0, 1), (2, 3)) if 0 in targets else ():
            @pl.when((g == 1) & (i == src))
            def _():
                if u == 0:
                    ready_for(d)
                col_copy(d, u).start()

    @pl.when((c == 1) | (g == 0))
    def _():
        local(0)

    for u in range(PER):
        arrival(row_in.at[pl.ds(0, 3), u], ri_r.at[u]).wait_recv()
        total = row_in[0, u]
        ahead[0, u] = jnp.zeros((width, width), F32)
        ahead[1, u] = total
        total = total + row_in[1, u]
        ahead[2, u] = total
        total = total + row_in[2, u]
        ahead[3, u] = total
        rowsum[u] = total + row_in[3, u]

        send_column(u, (0, 3))

    for u in range(PER):
        send_column(u, (2, 1))

    @pl.when((c == 1) & (g == 1))
    def _():
        local(1)


    def row_result(u):
        for off in (2, 1, 3):
            row_src[off, u] = offset[u] + ahead[row_place(px, off), u]
            row_back(off, u).start()
        row_out[px, u] = offset[u] + ahead[px, u]

    def takes(s):
        terms = (i == 1) if s == 0 else (i > 1) if s == 1 else (i == 3)
        return ((g == 0) & (s < i)) | ((g == 1) & terms)

    for u in range(PER):
        offset[u] = jnp.zeros((width, width), F32)
        for s in range(HALF - 1):
            @pl.when(takes(s))
            def _():
                arrival(col_in.at[s, u], z_r.at[s, u]).wait_recv()
                offset[u] += col_in[s, u]

        @pl.when((g == 1) & (i == 1))
        def _():
            pair_src[u] = offset[u] + rowsum[u]
            for d in (3, 2):
                if u == 0:
                    ready_for(d)
                pair_copy(d, u).start()

        @pl.when((g == 0) & (c == 0))
        def _():
            row_result(u)

    for u in range(PER):
        for end, due in ((0, ([(7, 0)], [(7, 1), (6, 1)])), (HALF - 1, ([(6, 0), (5, 0)], [(5, 1), (4, 0), (4, 1)]))):
            @pl.when((g == 0) & (i == end))
            def _():
                if end == 0:
                    for s in range(1, HALF):
                        arrival(col_in.at[s, u], z_r.at[s, u]).wait_recv()
                    half_src[u] = rowsum[u] + col_in[1, u] + col_in[2, u] + col_in[3, u]
                else:
                    half_src[u] = offset[u] + rowsum[u]
                for to, which in due[u]:
                    if which == 0 or to == 6:
                        @pl.when(c == 0)
                        def _():
                            pl.semaphore_wait(ready.at[to], 1)
                    half_copy(to, which).start()

    for u in range(PER):
        @pl.when(g == 1)
        def _():
            arrival(half_in.at[u], h_r.at[u]).wait_recv()
            offset[u] += half_in[u]

        @pl.when((g == 1) | (c == 1))
        def _():
            row_result(u)

    @pl.when(g == 0)
    def _():
        local(1)

    def emit(n, j, u, value):
        (gq, gk, gv)[n][j, u] = (part[n, j, u] + value).astype(BF16)

    def finish(kind, places, states_in):
        @pl.when(kind == 0)
        def _():
            for j, u in places:
                emit(0, j, u, dot(inb[3, j, u], states_in[j, u].astype(BF16), NT))

        @pl.when(kind == 1)
        def _():
            for j, u in places:
                state = states_in[j, u].astype(BF16)
                emit(1, j, u, dot(inb[1, j, u], state, NT))
                emit(2, j, u, dot(inb[0, j, u], state, NN))

    def own_kind():
        for u in range(PER):
            places = [(row_place(px, off), u) for off in (0, 1, 3, 2)]
            for off, (j, _) in zip((0, 1, 3, 2), places):
                if off:
                    arrival(row_out.at[j, u], ro_r.at[j, u]).wait_recv()
                core_src[j, u] = row_out[j, u] + own[j, u]
                core_back(j, u, off).start()
            finish(c, places, row_out)

    def other_kind():
        for u in range(PER):
            places = [(row_place(other_px, off), u) for off in (0, 1, 3, 2)]
            for batch in (places,) if u == 0 else (places[:3], places[3:]):
                last = u + 1 if len(batch) == 1 else u
                arrival(core_out.at[pl.ds(0, len(batch)), u], co_r.at[last]).wait_recv()
                finish(1 - c, batch, core_out)

    @pl.when(g == 1)
    def _():
        other_kind()

    own_kind()

    @pl.when(g == 0)
    def _():
        other_kind()

    def sent(ref, sem):
        remote(ref, ref, sem, sem, partner).wait_send()

    sent(away, ci_s)
    sent(chip.at[pl.ds(0, 3)], ri_s)
    sent(row_src.at[pl.ds(1, 3)], ro_s)
    sent(core_src, co_s)
    for d in range(HALF):
        back = ((i == 0) if d == 1 else (i == 1) if d == 2 else (i == 1) | (i == 2)) & (d > 0)
        forward = (d > i) | ((i > 0) & (d == 0))

        @pl.when(((g == 0) & forward) | ((g == 1) & back))
        def _():
            sent(rowsum, z_s.at[d])

    @pl.when((g == 0) & (i == 0))
    def _():
        sent(half_src.at[0], h_s.at[0])
        sent(half_src, h_s.at[1])

    @pl.when((g == 0) & (i == HALF - 1))
    def _():
        sent(row_src.at[pl.ds(1, 3), 0], h_s.at[0])
        sent(half_src, h_s.at[1])


def put(*refs):
    sources, targets, sems = refs[:3], refs[3:6], refs[6]
    copies = [
        pltpu.make_async_copy(sources[n], targets[n], sems.at[n])
        for n in range(3)
    ]
    for copy in copies:
        copy.start()
    for copy in copies:
        copy.wait()


def body(queries, key_rows, value_rows, grad_out):
    heads, tile, width = queries.shape
    split = (COLS, PER, tile, width)
    square = (width, width)
    sem = pltpu.SemaphoreType.DMA
    four = pltpu.VMEM((COLS, PER, *square), F32)
    two = pltpu.VMEM((PER, *square), F32)
    pairs = sem((COLS, PER))
    grads = pl.pallas_call(
        kernel,
        out_shape=[pltpu.VMEM(split, BF16)] * 3,
        in_specs=[pl.BlockSpec(memory_space=pl.ANY)] * 4,
        out_specs=[pl.BlockSpec(memory_space=pltpu.VMEM)] * 3,
        scratch_shapes=[
            pltpu.VMEM((4, *split), BF16),
            pltpu.VMEM((3, *split), F32),
            four, four, four, four, four, four, two, four, two, two, two, two,
            four, four, four, four,
            sem((4,)),
            sem, pairs, sem, sem((PER,)), sem((COLS,)), pairs, sem((PER,)), sem((PER,)), sem, pairs, sem, sem((PER + 1,)),
            pltpu.SemaphoreType.REGULAR((ROWS,)),
            pltpu.SemaphoreType.REGULAR,
        ],
        compiler_params=pltpu.CompilerParams(
            collective_id=0, has_side_effects=True, vmem_limit_bytes=61 * 2**20
        ),
    )(*(a.reshape(split) for a in (key_rows, value_rows, queries, grad_out)))
    grads = pl.pallas_call(
        put,
        out_shape=[jax.ShapeDtypeStruct(split, BF16)] * 3,
        in_specs=[pl.BlockSpec(memory_space=pl.ANY)] * 3,
        out_specs=[pl.BlockSpec(memory_space=pl.ANY)] * 3,
        scratch_shapes=[sem((3,))],
        compiler_params=pltpu.CompilerParams(vmem_limit_bytes=2**20),
    )(*grads)
    return tuple(a.reshape(heads, tile, width) for a in grads)


def solution(mesh):
    placed = P("head", "seq", None)
    return jax.shard_map(
        body, mesh=mesh, in_specs=(placed,) * 4, out_specs=(placed,) * 3, check_vma=False
    )
```

```python
import jax
import jax.numpy as jnp
from jax import lax
from jax.experimental import pallas as pl
from jax.experimental.pallas import tpu as pltpu
from jax.sharding import PartitionSpec as P

ROWS, COLS, PER = 8, 4, 2
HALF = ROWS // 2
F32, BF16 = jnp.float32, jnp.bfloat16
NN = (((1,), (0,)), ((), ()))
NT = (((1,), (1,)), ((), ()))
TN = (((0,), (0,)), ((), ()))


def dot(a, b, dims):
    return lax.dot_general(a, b, dims, preferred_element_type=F32)


def kernel(
    k_hbm, v_hbm, q_hbm, g_hbm,
    gq, gk, gv,
    inb, part, own, away, core_in, chip, row_in, ahead, rowsum, col_in, offset, half_src, half_in, pair_src,
    row_src, row_out, core_src, core_out,
    in_sem,
    ci_s, ci_r, ri_s, ri_r, z_s, z_r, h_s, h_r, ro_s, ro_r, co_s, co_r, ready, row_ready,
):
    tile, width = inb.shape[3:]
    place = lax.axis_index("seq")
    c = lax.rem(place, 2)
    x = lax.rem(lax.div(place, 2), COLS)
    z = lax.div(place, 2 * COLS)
    px = x + c * (COLS - 1 - 2 * x)
    p = z + c * (ROWS - 1 - 2 * z)
    g = lax.div(p, HALF)
    i = lax.rem(p, HALF)

    def device(pp, ppx):
        zz = pp + c * (ROWS - 1 - 2 * pp)
        xx = ppx + c * (COLS - 1 - 2 * ppx)
        return {"seq": (zz * COLS + xx) * 2 + c}

    partner = {"seq": place + 1 - 2 * c}

    def row_place(start, off):
        return lax.rem(start + off, COLS)

    barrier = pltpu.get_barrier_semaphore()

    def greet(peer):
        pl.semaphore_signal(barrier, inc=1, device_id=peer, device_id_type=pl.DeviceIdType.MESH)

    greet(partner)
    for off in (1, 2, 3):
        greet({"seq": (z * COLS + row_place(x, off)) * 2 + 1})
    first = lax.rem(z, HALF)
    for d in range(HALF):
        @pl.when(d > first)
        def _():
            zz = z - first + d
            greet({"seq": (zz * COLS + x) * 2 + c})

    for low, high, core in ((0, 7, 0), (0, 6, 0), (3, 4, 0), (3, 5, 0), (0, 7, 1), (1, 7, 1), (3, 4, 1), (2, 4, 1), (3, 6, 0), (1, 4, 1)):
        @pl.when((z == low) & (c == core))
        def _():
            greet({"seq": (high * COLS + x) * 2 + core})

    sources = (k_hbm, v_hbm, q_hbm, g_hbm)
    other_px = COLS - 1 - px

    def load(source, a, u):
        return pltpu.make_async_copy(source.at[:, u], inb.at[a, :, u], in_sem.at[a, u])

    for pair in ((2, 3), (0, 1)):
        for u in range(PER):
            for a in pair:
                load(sources[a], a, u).start()

    upper = lax.div(z, HALF)
    late_end = jnp.where(z == 7, 2, 0) + jnp.where(z == 4, 3, 0)
    column = upper + jnp.where(z == 6, 1, 0)
    expected = 1 + first + jnp.where(c == 0, column, 6 + late_end)

    def remote(src, dst, send, recv, peer):
        return pltpu.make_async_remote_copy(
            src_ref=src, dst_ref=dst, send_sem=send, recv_sem=recv, device_id=peer,
            device_id_type=pl.DeviceIdType.MESH,
        )

    def core_copy(j, u):
        return remote(away.at[j, u], core_in.at[j, u], ci_s, ci_r.at[j, u], partner)

    def row_copy(off, u):
        j = row_place(px, off)
        return remote(chip.at[j, u], row_in.at[px, u], ri_s, ri_r.at[u], device(p, j))

    def pair_copy(d, u):
        return remote(pair_src.at[u], col_in.at[1, u], z_s.at[d], z_r.at[1, u], device(g * HALF + d, px))

    def col_copy(d, u):
        return remote(rowsum.at[u], col_in.at[i, u], z_s.at[d], z_r.at[i, u], device(g * HALF + d, px))

    def half_copy(to, u):
        return remote(half_src.at[u], half_in.at[u], h_s.at[u], h_r.at[u], device(to, px))

    def row_back(off, u):
        j = row_place(px, off)
        return remote(row_src.at[off, u], row_out.at[px, u], ro_s, ro_r.at[px, u], device(p, j))

    def core_back(j, u, off):
        batch = u + 1 if u == 1 and off == 2 else u
        return remote(core_src.at[j, u], core_out.at[j, u], co_s, co_r.at[batch], partner)

    def arrival(ref, sem):
        return remote(ref, ref, sem, sem, partner)

    def states(kind, begin, into, which):
        places = [(row_place(begin, off), u) for u in which for off in (2, 1, 3, 0)]
        for u in which:
            for a in (2 * kind, 2 * kind + 1):
                load(sources[a], a, u).wait()
        for j, u in places:
            into[j, u] = dot(inb[2 * kind, j, u], inb[2 * kind + 1, j, u], TN)

    def hand_in(which):
        if 0 in which:
            pl.semaphore_wait(barrier, expected)
        for u in which:
            for off in (2, 1, 3, 0):
                core_copy(row_place(other_px, off), u).start()

    @pl.when(c == 0)
    def _():
        for u in range(PER):
            states(1, other_px, away, (u,))
            hand_in((u,))
        states(0, px, own, (0, 1))

    @pl.when(c == 1)
    def _():
        states(1, px, own, (0, 1))
        states(0, other_px, away, (0, 1))
        hand_in((0, 1))
        pl.semaphore_signal(row_ready, inc=1, device_id=partner, device_id_type=pl.DeviceIdType.MESH)

    def answer(sender):
        pl.semaphore_signal(
            ready.at[p], inc=1, device_id=device(sender, px), device_id_type=pl.DeviceIdType.MESH
        )

    for s in range(HALF):
        @pl.when((c == 0) & (g == 0) & (s < i))
        def _():
            answer(s)

        @pl.when((c == 1) & (p == 0) & (s > 0))
        def _():
            answer(s)

    @pl.when((c == 0) & (g == 1))
    def _():
        answer(jnp.where(i < 2, HALF - 1, 0))

    @pl.when((c == 0) & (p == 6))
    def _():
        answer(HALF - 1)

    for src, d in ((0, 1), (0, 2), (1, 2), (1, 3), (2, 3)):
        @pl.when((c == 0) & (g == 1) & (i == d))
        def _():
            answer(HALF + src)

    causal = lax.broadcasted_iota(jnp.int32, (tile, tile), 0) >= lax.broadcasted_iota(jnp.int32, (tile, tile), 1)

    def local(half):
        @pl.loop(0, COLS)
        def _(n):
            j, u = half * 2 + lax.div(n, 2), lax.rem(n, 2)
            k, v, q, go = (inb[a, j, u] for a in range(4))
            scores = jnp.where(causal, dot(go, v, NT), 0.0).astype(BF16)
            part[0, j, u] = dot(scores, k, NN)
            part[1, j, u] = dot(scores, q, TN)
            scores = jnp.where(causal, dot(q, k, NT), 0.0).astype(BF16)
            part[2, j, u] = dot(scores, go, TN)

    @pl.when((c == 0) & (g == 1))
    def _():
        local(0)
        local(1)

    @pl.when(c == 0)
    def _():
        pl.semaphore_wait(row_ready, 1)

    for u in range(PER):
        for off in (2, 1, 3, 0):
            j = row_place(px, off)
            core_copy(j, u).wait_recv()
            if off:
                chip[j, u] = own[j, u] + core_in[j, u]
                row_copy(off, u).start()
            else:
                row_in[px, u] = own[px, u] + core_in[px, u]

    def ready_for(d):
        @pl.when((c == 0) == (d > i))
        def _():
            pl.semaphore_wait(ready.at[g * HALF + d], 1)

    def send_column(u, targets):
        for d in targets:
            @pl.when((g == 0) & ((d > i) | ((i > 0) & (d == 0))))
            def _():
                if u == 0:
                    ready_for(d)
                col_copy(d, u).start()

        for src, d in ((0, 1), (0, 2), (1, 2), (2, 3)) if 0 in targets else ():
            @pl.when((g == 1) & (i == src) & ((c == 0) | (d != 2)))
            def _():
                if u == 0:
                    ready_for(d)
                col_copy(d, u).start()

    @pl.when((c == 1) | (g == 0))
    def _():
        local(0)

    for u in range(PER):
        arrival(row_in.at[pl.ds(0, 3), u], ri_r.at[u]).wait_recv()
        total = row_in[0, u]
        ahead[0, u] = jnp.zeros((width, width), F32)
        ahead[1, u] = total
        total = total + row_in[1, u]
        ahead[2, u] = total
        total = total + row_in[2, u]
        ahead[3, u] = total
        rowsum[u] = total + row_in[3, u]

        send_column(u, (0, 3))

    for u in range(PER):
        send_column(u, (2, 1))

    @pl.when((c == 1) & (g == 1))
    def _():
        local(1)


    def row_result(u):
        for off in (2, 1, 3):
            row_src[off, u] = offset[u] + ahead[row_place(px, off), u]
            row_back(off, u).start()
        row_out[px, u] = offset[u] + ahead[px, u]

    def takes(s):
        terms = (i == 1) | ((i == 2) & (c == 0)) if s == 0 else (i > 1) if s == 1 else (i == 3)
        return ((g == 0) & (s < i)) | ((g == 1) & terms)

    for u in range(PER):
        offset[u] = jnp.zeros((width, width), F32)
        for s in range(HALF - 1):
            @pl.when(takes(s))
            def _():
                arrival(col_in.at[s, u], z_r.at[s, u]).wait_recv()
                offset[u] += col_in[s, u]

        @pl.when((g == 1) & (i == 1))
        def _():
            pair_src[u] = offset[u] + rowsum[u]
            if u == 0:
                ready_for(3)
            pair_copy(3, u).start()

            @pl.when(c == 1)
            def _():
                pair_copy(2, u).start()

        @pl.when((g == 0) & (c == 0))
        def _():
            row_result(u)

    for u in range(PER):
        for end, due in ((0, ([(7, 0)], [(7, 1), (6, 1)])), (HALF - 1, ([(6, 0), (5, 0)], [(5, 1), (4, 0), (4, 1)]))):
            @pl.when((g == 0) & (i == end))
            def _():
                if end == 0:
                    for s in range(1, HALF):
                        arrival(col_in.at[s, u], z_r.at[s, u]).wait_recv()
                    half_src[u] = rowsum[u] + col_in[1, u] + col_in[2, u] + col_in[3, u]
                else:
                    half_src[u] = offset[u] + rowsum[u]
                for to, which in due[u]:
                    if which == 0 or to == 6:
                        @pl.when(c == 0)
                        def _():
                            pl.semaphore_wait(ready.at[to], 1)
                    half_copy(to, which).start()

    for u in range(PER):
        @pl.when(g == 1)
        def _():
            arrival(half_in.at[u], h_r.at[u]).wait_recv()
            offset[u] += half_in[u]

        @pl.when((g == 1) | (c == 1))
        def _():
            row_result(u)

    @pl.when(g == 0)
    def _():
        local(1)

    def emit(n, j, u, value):
        (gq, gk, gv)[n][j, u] = (part[n, j, u] + value).astype(BF16)

    def finish(kind, places, states_in):
        @pl.when(kind == 0)
        def _():
            for j, u in places:
                emit(0, j, u, dot(inb[3, j, u], states_in[j, u].astype(BF16), NT))

        @pl.when(kind == 1)
        def _():
            for j, u in places:
                state = states_in[j, u].astype(BF16)
                emit(1, j, u, dot(inb[1, j, u], state, NT))
                emit(2, j, u, dot(inb[0, j, u], state, NN))

    def own_kind():
        for u in range(PER):
            places = [(row_place(px, off), u) for off in (0, 1, 3, 2)]
            for off, (j, _) in zip((0, 1, 3, 2), places):
                if off:
                    arrival(row_out.at[j, u], ro_r.at[j, u]).wait_recv()
                core_src[j, u] = row_out[j, u] + own[j, u]
                core_back(j, u, off).start()
            finish(c, places, row_out)

    def other_kind():
        for u in range(PER):
            places = [(row_place(other_px, off), u) for off in (0, 1, 3, 2)]
            for batch in (places,) if u == 0 else (places[:3], places[3:]):
                last = u + 1 if len(batch) == 1 else u
                arrival(core_out.at[pl.ds(0, len(batch)), u], co_r.at[last]).wait_recv()
                finish(1 - c, batch, core_out)

    @pl.when(g == 1)
    def _():
        other_kind()

    own_kind()

    @pl.when(g == 0)
    def _():
        other_kind()

    def sent(ref, sem):
        remote(ref, ref, sem, sem, partner).wait_send()

    sent(away, ci_s)
    sent(chip.at[pl.ds(0, 3)], ri_s)
    sent(row_src.at[pl.ds(1, 3)], ro_s)
    sent(core_src, co_s)
    for d in range(HALF):
        back = ((i == 0) if d == 1 else (i == 1) | ((i == 0) & (c == 0)) if d == 2 else (i == 1) | (i == 2)) & (d > 0)
        forward = (d > i) | ((i > 0) & (d == 0))

        @pl.when(((g == 0) & forward) | ((g == 1) & back))
        def _():
            sent(rowsum, z_s.at[d])

    @pl.when((g == 0) & (i == 0))
    def _():
        sent(half_src.at[0], h_s.at[0])
        sent(half_src, h_s.at[1])

    @pl.when((g == 0) & (i == HALF - 1))
    def _():
        sent(row_src.at[pl.ds(1, 3), 0], h_s.at[0])
        sent(half_src, h_s.at[1])


def put(*refs):
    sources, targets, sems = refs[:3], refs[3:6], refs[6]
    copies = [
        pltpu.make_async_copy(sources[n], targets[n], sems.at[n])
        for n in range(3)
    ]
    for copy in copies:
        copy.start()
    for copy in copies:
        copy.wait()


def body(queries, key_rows, value_rows, grad_out):
    heads, tile, width = queries.shape
    split = (COLS, PER, tile, width)
    square = (width, width)
    sem = pltpu.SemaphoreType.DMA
    four = pltpu.VMEM((COLS, PER, *square), F32)
    two = pltpu.VMEM((PER, *square), F32)
    pairs = sem((COLS, PER))
    grads = pl.pallas_call(
        kernel,
        out_shape=[pltpu.VMEM(split, BF16)] * 3,
        in_specs=[pl.BlockSpec(memory_space=pl.ANY)] * 4,
        out_specs=[pl.BlockSpec(memory_space=pltpu.VMEM)] * 3,
        scratch_shapes=[
            pltpu.VMEM((4, *split), BF16),
            pltpu.VMEM((3, *split), F32),
            four, four, four, four, four, four, two, four, two, two, two, two,
            four, four, four, four,
            sem((4, PER)),
            sem, pairs, sem, sem((PER,)), sem((COLS,)), pairs, sem((PER,)), sem((PER,)), sem, pairs, sem, sem((PER + 1,)),
            pltpu.SemaphoreType.REGULAR((ROWS,)),
            pltpu.SemaphoreType.REGULAR,
        ],
        compiler_params=pltpu.CompilerParams(
            collective_id=0, has_side_effects=True, vmem_limit_bytes=61 * 2**20
        ),
    )(*(a.reshape(split) for a in (key_rows, value_rows, queries, grad_out)))
    grads = pl.pallas_call(
        put,
        out_shape=[jax.ShapeDtypeStruct(split, BF16)] * 3,
        in_specs=[pl.BlockSpec(memory_space=pl.ANY)] * 3,
        out_specs=[pl.BlockSpec(memory_space=pl.ANY)] * 3,
        scratch_shapes=[sem((3,))],
        compiler_params=pltpu.CompilerParams(vmem_limit_bytes=2**20),
    )(*grads)
    return tuple(a.reshape(heads, tile, width) for a in grads)


def solution(mesh):
    placed = P("head", "seq", None)
    return jax.shard_map(
        body, mesh=mesh, in_specs=(placed,) * 4, out_specs=(placed,) * 3, check_vma=False
    )
```
